32 devices in a mesh: blk: 16 (over z, y, x), grp: 2 (over core).
Axes of the slice: x: 2, y: 2, z: 4, core: 2. Of those that a mesh axis runs over, the one named last changes fastest.
Arguments:
- atom_value: float32 [512, 128], P('blk'), may hold values from 0 to 1
- target_value: float32 [512, 128], P('blk'), may hold values from 0 to 1
- observed: int32 [512, 128], P('blk'), may hold values 0 or 1
- block_owner: int32 [1024, 4], replicated, may hold values from 0 to 15, all different within a row; in each aligned block of 64 rows (0 to 63, 64 to 127, ...) at most 32 rows name the same one
- block_local: int32 [1024, 4], replicated, may hold values from 0 to 31
- slot_index: int32 [3, 2, 131072], P(None, 'grp', 'blk'), may hold values from 0 to 512, as said below
- coefficient: float32 [3, 2, 131072], P(None, 'grp', 'blk'), may hold values from -1.5 to 1.5, as said below
- offset: float32 [2, 131072], P('grp', 'blk'), may hold values from -1 to 0.5
- dual_value: float32 [3, 2, 131072], P(None, 'grp', 'blk'), may hold values from -1.5 to 1.5
- template: int32 [2, 1024], P('grp', 'blk'), may hold values from 0 to 19
- weight: float32 [40], replicated, may hold values from 0.5 to 4
Outputs:
- consensus: float32 [512, 128], P('blk')
- dual_next: float32 [3, 2, 131072], P(None, 'grp', 'blk')
- weight_next: float32 [40], replicated
The draws below stay inside these ranges and needn't reach their ends.
Inputs may be any that keep to these rules, and one draw needn't show every extreme that they name: `block_owner`: each tile lists 4 different owners; in each aligned block of 64 tiles no owner is listed more than 32 times. `slot_index`: the value 4 * 128 marks an unused slot; slots 0 and 1 of every rule are in use. `coefficient`: every magnitude is 0.5 or more.
All inputs are finite; a program needn't handle non-finite values. No bound on the sum of `observed` on one device may be relied on, other than what follows from the above.
Results may differ from the reference program's by a relative error of at most 0.00026.
Values sent between devices are 32-bit elements; how exact they have to be, the bound alone decides.
No kernel may reach another device: no remote copies, remote signals or barrier semaphores. Data moves between devices by JAX's collectives and lax.ppermute only.
A program may use at most 64 MiB of HBM per device.

```python
import math
import jax
import jax.numpy as jnp
import numpy as np

AB = 128
K = 4
ARITY = 3
TEMPL = 40
ITERS = 2
ATOM_BLK = 32
TILE_DEV = 64
CAP = 32
NBLOCKS = 512
TILES = 1024
ROWS = 131072
PER_GROUP = 20
N_BLK = 16
N_GRP = 2


def draw_slot_index(key, part):
    key_pick, key_drop = jax.random.split(key)
    picked = jax.random.randint(key_pick, (ARITY, N_GRP, ROWS), 0, K * AB)
    dropped = jax.random.randint(key_drop, (ARITY, N_GRP, ROWS), 0, 3) == 0
    last_slot = jnp.arange(ARITY)[:, None, None] >= 2
    return jnp.where(dropped & last_slot, K * AB, picked).astype(jnp.int32)


def draw_coefficient(key, part):
    key_size, key_sign = jax.random.split(key)
    uniform_part = jax.random.uniform(key_size, (ARITY, N_GRP, ROWS), jnp.float32)
    magnitude = 0.5 + uniform_part
    sign_value = jnp.where(jax.random.bernoulli(key_sign, 0.5, (ARITY, N_GRP, ROWS)), 1.0, -1.0)
    return (sign_value * magnitude).astype(jnp.float32)


def with_ends(result, rng, least, largest):
    extent = result.shape
    place = [jax.random.randint(jax.random.fold_in(rng, axis), (), 0, extent[axis]) for axis in range(len(extent))]
    result = result.at[tuple(place)].set(least)
    longest = extent.index(max(extent))
    place[longest] = (place[longest] + 1) % extent[longest]
    return result.at[tuple(place)].set(largest)


def shard_levels(rng, shape, cuts, least, top_value):
    gain, own = 1.0, jax.random.fold_in(rng, 6)
    for dim, blocks in cuts:
        heights = jnp.exp(jax.random.uniform(jax.random.fold_in(own, dim), (blocks,), jnp.float32, least / len(cuts), top_value / len(cuts)))
        gain = gain * jnp.repeat(heights, shape[dim] // blocks).reshape([-1 if axis == dim else 1 for axis in range(len(shape))])
    return gain


def assign_block(own_key, own, number, rows, count, top, limit, lean):
    order = jax.random.permutation(own_key, count)
    crowded, usual = portions_of(count, rows * top, limit, lean, True), portions_of(count, rows * top, limit, lean, False)
    places = jnp.arange(count)

    def named(lengths, rotation):
        used = int((lengths > 0).sum())
        fixed = max(1, used // 4)
        moved = fixed + (places - fixed + rotation * (used - fixed)) % max(1, count - fixed)
        return jnp.zeros((count,), jnp.int32).at[order[jnp.where(places < fixed, places, moved)]].set(jnp.asarray(lengths, jnp.int32))

    lengths = jnp.where(number % 4 == 0, named(crowded, number // 4), named(usual, number - number // 4 - 1))
    mixed = jax.random.permutation(jax.random.fold_in(own, 3), count)
    source_of, receiver = mixed[0:count // 2 * 2:2], mixed[1:count // 2 * 2:2]
    margin = jnp.minimum(lengths[source_of] - 1, limit - lengths[receiver]) // 2
    margin = jnp.where((source_of == order[0]) | (receiver == order[0]) | (lengths[receiver] == 0), 0, jnp.maximum(margin, 0))
    moved = jax.random.randint(jax.random.fold_in(own, 4), (count // 2,), 0, 1 << 20) % (margin + 1)
    lengths = lengths.at[source_of].add(-moved).at[receiver].add(moved)
    labels = jnp.searchsorted(jnp.cumsum(lengths), jnp.arange(rows * top), side="right").astype(jnp.int32)
    listing = labels.reshape(top, rows).T
    listing = listing[jax.random.permutation(jax.random.fold_in(own, 1), rows)]
    rotation = jax.random.randint(jax.random.fold_in(own, 2), (rows, 1), 0, top)
    return jnp.take_along_axis(listing, (jnp.arange(top)[None, :] + rotation) % top, axis=1)


def portions_of(count, total, limit, skew, full):
    portions = [(1 << 20) // math.isqrt(standing ** skew) + 1 for standing in range(1, count + 1)]
    largest = limit if full else min(limit, max(-(-total // count), total * portions[0] // sum(portions)))
    least = 1 if total - largest >= count - 1 else 0
    given, spare = [largest] + [least] * (count - 1), total - largest - least * (count - 1)
    while spare > 0:
        free = [i for i in range(1, count) if given[i] < largest] or [i for i in range(1, count) if given[i] < limit]
        pool, remaining = sum([portions[i] for i in free]), spare
        for i in free:
            more = min(limit - given[i], max(1, remaining * portions[i] // pool), spare)
            given[i] = given[i] + more
            spare = spare - more
    return np.array(given)


def normal_values(key, shape, width, reach, shards=(), held_as=jnp.bfloat16):
    result = width * jax.random.normal(key, shape, jnp.float32)
    if shards:
        result = result * shard_levels(key, shape, shards, -0.22, 0.18)
    return jnp.clip(result, -reach, reach).astype(held_as)


def setup_inputs(seed: int = 0) -> dict:
    key_list = jax.random.split(jax.random.key(seed), 12)
    atom_value = jnp.clip(1.0 * jax.random.uniform(key_list[0], (NBLOCKS, AB), jnp.float32) ** shard_levels(key_list[0], (NBLOCKS, AB), ((0, 16),), -0.2, 0.2), 0.0, 1.0)
    target_value = jnp.clip(1.0 * jax.random.uniform(key_list[1], (NBLOCKS, AB), jnp.float32) ** shard_levels(key_list[1], (NBLOCKS, AB), ((0, 16),), -0.2, 0.2), 0.0, 1.0)
    observed = with_ends((jax.random.randint(key_list[2], (NBLOCKS, AB), 0, 4) < 1).astype(jnp.int32), jax.random.fold_in(key_list[2], 1), 0, 1)
    block_owner_keys = jax.random.split(jax.random.fold_in(key_list[3], 1), TILES // TILE_DEV)
    block_owner_turns = jax.random.permutation(jax.random.fold_in(key_list[3], 3), TILES // TILE_DEV)
    block_owner = jax.vmap(lambda own, number: assign_block(jax.random.fold_in(key_list[3], 2), own, number, TILE_DEV, N_BLK, K, CAP, 2))(block_owner_keys, block_owner_turns).reshape((TILES, K))
    block_local = with_ends(jax.random.randint(key_list[4], (TILES, K), 0, ATOM_BLK), jax.random.fold_in(key_list[4], 1), 0, ATOM_BLK - 1).astype(jnp.int32)
    slot_index = draw_slot_index(jax.random.fold_in(key_list[11], 71), 0)
    coefficient = draw_coefficient(jax.random.fold_in(key_list[11], 71), 0)
    offset = jnp.clip(-1.0 + 1.5 * jax.random.uniform(key_list[7], (N_GRP, ROWS), jnp.float32) ** shard_levels(key_list[7], (N_GRP, ROWS), ((0, 2), (1, 16)), -0.2, 0.2), -1.0, 0.5)
    dual_value = normal_values(key_list[8], (ARITY, N_GRP, ROWS), 0.3, 1.5, ((1, 2), (2, 16)), jnp.float32)
    template = with_ends(jax.random.randint(key_list[9], (N_GRP, TILES), 0, PER_GROUP), jax.random.fold_in(key_list[9], 1), 0, PER_GROUP - 1).astype(jnp.int32)
    weight = jnp.clip(jnp.exp(jax.random.uniform(key_list[10], (TEMPL,), jnp.float32, math.log(0.5), math.log(4.0))), 0.5, 4.0)
    return dict(atom_value=atom_value, target_value=target_value, observed=observed, block_owner=block_owner, block_local=block_local, slot_index=slot_index, coefficient=coefficient, offset=offset, dual_value=dual_value, template=template, weight=weight)


PENALTY = 1.0
LEARN_RATE = 2.0


def reference(atom_value, target_value, observed, block_owner, block_local, slot_index, coefficient, offset, dual_value, template, weight):
    atoms_all = NBLOCKS * AB
    window_len = K * AB
    current = atom_value.reshape(-1)
    targets = target_value.reshape(-1)
    fixed_mask = observed.reshape(-1) == 1
    blocks = (block_owner * ATOM_BLK + block_local).astype(jnp.int32)
    row_tile = (jnp.arange(ROWS, dtype=jnp.int32) // AB).astype(jnp.int32)
    in_use = slot_index < window_len
    clipped = jnp.minimum(slot_index, window_len - 1)
    atom_index = (blocks[row_tile[None, None, :], clipped // AB] * AB + clipped % AB).astype(jnp.int32)
    active = jnp.where(in_use, coefficient, jnp.float32(0.0))
    norm_sq = jnp.sum(active * active, axis=0)
    templates = (jnp.arange(N_GRP, dtype=jnp.int32)[:, None] * (TEMPL // N_GRP) + template).astype(jnp.int32)
    row_templ = templates[:, row_tile]
    row_weight = weight[row_templ]
    squared = row_templ % 2 == 1
    flat_index = atom_index.reshape(-1)
    use_flat = in_use.reshape(-1).astype(jnp.float32)

    def fetch(values):
        return jnp.where(in_use, values[atom_index], jnp.float32(0.0))

    def hinge_step(copies, duals):
        shifted = copies - duals
        linear_part = offset + jnp.sum(active * shifted, axis=0)
        plain_step = jnp.clip(linear_part / norm_sq, 0.0, row_weight / PENALTY)
        square_step = 2.0 * row_weight * jnp.maximum(linear_part, 0.0) / (PENALTY + 2.0 * row_weight * norm_sq)
        chosen = jnp.where(squared, square_step, plain_step)
        return shifted - chosen[None] * active

    def energy(copies):
        linear_part = offset + jnp.sum(active * copies, axis=0)
        positive = jnp.maximum(linear_part, 0.0)
        row_energy = jnp.where(squared, positive * positive, positive)
        return jax.ops.segment_sum(row_energy.reshape(-1), row_templ.reshape(-1), num_segments=TEMPL)

    counts = jax.ops.segment_sum(use_flat, flat_index, num_segments=atoms_all)
    values = current
    duals = dual_value
    moved = dual_value
    for sweep in range(ITERS):
        copies = fetch(values)
        if sweep > 0:
            duals = duals + jnp.where(in_use, moved - copies, jnp.float32(0.0))
        moved = hinge_step(copies, duals)
        sums = jax.ops.segment_sum(jnp.where(in_use, moved + duals, jnp.float32(0.0)).reshape(-1), flat_index, num_segments=atoms_all)
        values = jnp.where(fixed_mask, current, jnp.clip((sums + values) / (counts + 1.0), 0.0, 1.0))
    copies = fetch(values)
    dual_next = duals + jnp.where(in_use, moved - copies, jnp.float32(0.0))
    e_value = energy(copies)
    e_target = energy(fetch(targets))
    weight_next = weight * jnp.exp(-LEARN_RATE * (e_value - e_target) / (e_value + e_target + 1.0))
    return values.reshape(NBLOCKS, AB), dual_next, weight_next
```

```python
import jax
import jax.numpy as jnp
from jax import lax
from jax.experimental import pallas as pl
from jax.experimental.pallas import tpu as pltpu
from jax.sharding import PartitionSpec as P

TEMPL = 40
PENALTY = 1.0
LEARN_RATE = 2.0
GROUP = 8
VMEM = pltpu.VMEM
SMEM = pltpu.SMEM


def bits_of(count):
    bits, bit = [], 1
    while bit < count:
        bits.append(bit)
        bit *= 2
    return bits


def swap_cores(value):
    return lax.ppermute(value, "grp", [(0, 1), (1, 0)])


def exchange(value, steps, count):
    perm = [
        (2 * b + core, 2 * (b ^ steps[core]) + core) for b in range(count) for core in range(2)
    ]
    return lax.ppermute(value, ("blk", "grp"), perm)


def all_sum(value, count):
    bits = bits_of(count)
    half = len(bits) // 2
    turned = bits[half:] + bits[:half]
    for steps in zip(bits, turned):
        value = value + exchange(value, steps, count)
    return value


def row_of(row, height, width):
    return jnp.broadcast_to(row, (height, width))


def refresh(total, before, counted, observed):
    moved = jnp.clip((total + before) / (counted + 1.0), 0.0, 1.0)
    return jnp.where(observed > 0.5, before, moved)


def load_windows(place_ref, field_ref, window_ref, tiles, list_len):
    @pl.loop(0, tiles // GROUP)
    def _(group):
        base = pl.multiple_of(group * GROUP, GROUP)
        for i in range(GROUP):
            for k in range(list_len):
                spot = place_ref[(base + i) * list_len + k]
                window_ref[k, pl.ds(base + i, 1), :] = field_ref[pl.ds(spot, 1), :]


def fetch_rows(window_ref, rows, slot, list_len, width):
    lane = slot & (width - 1)
    which = slot // width
    result = jnp.zeros(slot.shape, jnp.float32)
    for k in range(list_len):
        taken = jnp.take_along_axis(window_ref[k, rows, :], lane, axis=1, mode="promise_in_bounds")
        result = jnp.where(which == k, taken, result)
    return result


def split_three(value):
    first = value.astype(jnp.bfloat16).astype(jnp.float32)
    rest = value - first
    second = rest.astype(jnp.bfloat16).astype(jnp.float32)
    return first, second, rest - second


def scatter_tile(place_ref, sum_ref, tile, lanes, whichs, values, list_len, width):
    hot, left = [], []
    pieces = len(values[0])
    height = 16
    row = lax.broadcasted_iota(jnp.int32, (height, width), 0)
    spot = lax.broadcasted_iota(jnp.int32, (width, width), 0)
    for lane, which, parts in zip(lanes, whichs, values):
        hot.append((row_of(lane, width, width) == spot).astype(jnp.float32).astype(jnp.bfloat16))
        value = row_of(parts[-1], height, width)
        for j in range(pieces - 2, -1, -1):
            value = jnp.where(row // list_len == j, row_of(parts[j], height, width), value)
        keep = row_of(which, height, width) == row % list_len
        keep = keep & (row < pieces * list_len)
        left.append(jnp.where(keep, value, 0.0).astype(jnp.bfloat16))
    summed = lax.dot_general(
        jnp.concatenate(left, axis=1),
        jnp.concatenate(hot, axis=1),
        (((1,), (1,)), ((), ())),
        preferred_element_type=jnp.float32,
    )
    total = summed[0:list_len]
    for j in range(1, pieces):
        total = total + summed[j * list_len : (j + 1) * list_len]
    spots = [place_ref[tile * list_len + k] for k in range(list_len)]
    olds = [sum_ref[pl.ds(at, 1), :] for at in spots]
    for k, at in enumerate(spots):
        sum_ref[pl.ds(at, 1), :] = olds[k] + total[k : k + 1]


def count_kernel(place_ref, slot_ref, keep_ref, send_ref, sum_ref, *, list_len):
    arity, tiles, width = slot_ref.shape
    half = keep_ref.shape[0]
    sum_ref[...] = jnp.zeros_like(sum_ref)

    @pl.loop(0, tiles // GROUP)
    def _(group):
        base = pl.multiple_of(group * GROUP, GROUP)
        rows = pl.ds(base, GROUP)
        slots = [slot_ref[s, rows, :] for s in range(arity)]
        one = jnp.ones((1, width), jnp.float32)
        for i in range(GROUP):
            scatter_tile(
                place_ref,
                sum_ref,
                base + i,
                [q[i : i + 1] & (width - 1) for q in slots],
                [q[i : i + 1] // width for q in slots],
                [(one,)] * arity,
                list_len,
                width,
            )

    keep_ref[...] = sum_ref[:half]
    send_ref[...] = sum_ref[half:]


def sweep_kernel(*refs, list_len, first):
    if first:
        (place_ref, field_ref, slot_ref, coef_ref, off_ref, dual_ref, temp_ref, weight_ref,
         moved_ref, keep_ref, send_ref, window_ref, sum_ref) = refs
    else:
        (place_ref, mine_ref, other_ref, before_ref, counted_ref, observed_ref,
         slot_ref, coef_ref, off_ref, dual_ref, old_ref, temp_ref, weight_ref,
         moved_ref, next_ref, field_ref, keep_ref, send_ref, window_ref, sum_ref) = refs
    arity, tiles, width = slot_ref.shape
    half = keep_ref.shape[0]
    if not first:
        for part, source in ((slice(0, half), mine_ref), (slice(half, None), other_ref)):
            field_ref[part] = refresh(
                source[...], before_ref[part], counted_ref[part], observed_ref[part]
            )
    load_windows(place_ref, field_ref, window_ref, tiles, list_len)
    sum_ref[...] = jnp.zeros_like(sum_ref)

    @pl.loop(0, tiles // GROUP)
    def _(group):
        base = pl.multiple_of(group * GROUP, GROUP)
        rows = pl.ds(base, GROUP)
        templ = temp_ref[rows, :]
        templates = weight_ref.shape[1]
        hot = row_of(templ, GROUP, templates) == lax.broadcasted_iota(
            jnp.int32, (GROUP, templates), 1
        )
        weight = jnp.sum(
            jnp.where(hot, row_of(weight_ref[...], GROUP, templates), 0.0), axis=1, keepdims=True
        )
        weight = jnp.broadcast_to(weight, (GROUP, width))
        squared = jnp.broadcast_to(templ % 2 == 1, (GROUP, width))
        slots = [slot_ref[s, rows, :] for s in range(arity)]
        used = [q < list_len * width for q in slots]
        acts = [jnp.where(used[s], coef_ref[s, rows, :], 0.0) for s in range(arity)]
        copies = [fetch_rows(window_ref, rows, q, list_len, width) for q in slots]
        duals = [dual_ref[s, rows, :] for s in range(arity)]
        if not first:
            duals = [
                d + jnp.where(m, old_ref[s, rows, :] - c, 0.0)
                for s, (d, m, c) in enumerate(zip(duals, used, copies))
            ]
            for s in range(arity):
                next_ref[s, rows, :] = duals[s]
        shifted = [c - d for c, d in zip(copies, duals)]
        linear = sum(a * v for a, v in zip(acts, shifted)) + off_ref[rows, :]
        norm = sum(a * a for a in acts)
        plain = jnp.clip(linear / norm, 0.0, weight / PENALTY)
        square = 2.0 * weight * jnp.maximum(linear, 0.0) / (PENALTY + 2.0 * weight * norm)
        chosen = jnp.where(squared, square, plain)
        parts = []
        for s in range(arity):
            moved = shifted[s] - chosen * acts[s]
            moved_ref[s, rows, :] = moved
            parts.append(split_three(jnp.where(used[s], moved + duals[s], 0.0)))
        for i in range(GROUP):
            scatter_tile(
                place_ref,
                sum_ref,
                base + i,
                [q[i : i + 1] & (width - 1) for q in slots],
                [q[i : i + 1] // width for q in slots],
                [tuple(p[i : i + 1] for p in part) for part in parts],
                list_len,
                width,
            )

    keep_ref[...] = sum_ref[:half]
    send_ref[...] = sum_ref[half:]


def energy_kernel(*refs, list_len, last):
    if last:
        (place_ref, own_ref, mine_ref, other_ref, before_ref, counted_ref, observed_ref,
         slot_ref, coef_ref, off_ref, dual_ref, old_ref, temp_ref, weight_ref,
         energy_ref, next_ref, owned_ref, window_ref, field_ref) = refs
    else:
        (place_ref, field_ref, slot_ref, coef_ref, off_ref, temp_ref, weight_ref,
         energy_ref, window_ref) = refs
    arity, tiles, width = slot_ref.shape
    templates = weight_ref.shape[1]
    if last:
        half = mine_ref.shape[0]
        for part, source in ((slice(0, half), mine_ref), (slice(half, None), other_ref)):
            field_ref[part] = refresh(
                source[...], before_ref[part], counted_ref[part], observed_ref[part]
            )
        piece = owned_ref.shape[0] // 2
        for h in range(2):
            start = pl.multiple_of(own_ref[h], GROUP)
            owned_ref[h * piece : (h + 1) * piece] = field_ref[pl.ds(start, piece), :]
    load_windows(place_ref, field_ref, window_ref, tiles, list_len)

    def step(group, total):
        base = pl.multiple_of(group * GROUP, GROUP)
        rows = pl.ds(base, GROUP)
        templ = temp_ref[rows, :]
        hot = row_of(templ, GROUP, templates) == lax.broadcasted_iota(
            jnp.int32, (GROUP, templates), 1
        )
        squared = jnp.broadcast_to(templ % 2 == 1, (GROUP, width))
        linear = off_ref[rows, :]
        for s in range(arity):
            slot = slot_ref[s, rows, :]
            used = slot < list_len * width
            copy = fetch_rows(window_ref, rows, slot, list_len, width)
            linear = linear + jnp.where(used, coef_ref[s, rows, :], 0.0) * copy
            if last:
                next_ref[s, rows, :] = dual_ref[s, rows, :] + jnp.where(
                    used, old_ref[s, rows, :] - copy, 0.0
                )
        positive = jnp.maximum(linear, 0.0)
        rule = jnp.where(squared, positive * positive, positive)
        tile = jnp.sum(rule, axis=1, keepdims=True)
        return total + jnp.where(hot, jnp.broadcast_to(tile, (GROUP, templates)), 0.0)

    total = lax.fori_loop(
        0, tiles // GROUP, step, jnp.zeros((GROUP, templates), jnp.float32)
    )
    energy_ref[...] = jnp.sum(total, axis=0, keepdims=True)


def specs(count, scalars):
    return [pl.BlockSpec(memory_space=SMEM)] * scalars + [
        pl.BlockSpec(memory_space=VMEM)
    ] * (count - scalars)


def call(body, args, scalars, outs, scratch):
    shapes = tuple(jax.ShapeDtypeStruct(s, jnp.float32) for s in outs)
    return pl.pallas_call(
        body,
        out_shape=shapes,
        in_specs=specs(len(args), scalars),
        out_specs=tuple(specs(len(outs), 0)),
        scratch_shapes=[VMEM(s, jnp.float32) for s in scratch],
    )(*args)


def local(
    atom_value,
    target_value,
    observed,
    block_owner,
    block_local,
    slot_index,
    coefficient,
    offset,
    dual_value,
    template,
    weight,
):
    device = lax.axis_index("blk")
    count = lax.axis_size("blk")
    core = lax.axis_index("grp")
    groups = lax.axis_size("grp")
    atom_blk, width = atom_value.shape
    tiles = template.shape[1]
    list_len = block_owner.shape[1]
    arity = slot_index.shape[0]
    piece = atom_blk // 2
    half = count * piece
    bits = bits_of(count)
    middle = len(bits) // 2
    order = bits[middle:] + bits[:middle]

    def position(owner):
        return sum(((owner // bit) % 2) << j for j, bit in enumerate(order))

    def place_of(owner, spot):
        return ((spot // piece) ^ core) * half + position(owner) * piece + spot % piece

    start = device * tiles
    place = place_of(
        lax.dynamic_slice_in_dim(block_owner, start, tiles, 0),
        lax.dynamic_slice_in_dim(block_local, start, tiles, 0),
    ).reshape(-1)
    own = place_of(device, jnp.arange(2, dtype=jnp.int32) * piece)
    slots = slot_index.reshape(arity, tiles, width)
    coeffs = coefficient.reshape(arity, tiles, width)
    offsets = offset.reshape(tiles, width)
    duals = dual_value.reshape(arity, tiles, width)
    templates = (core * (TEMPL // groups) + template[0])[:, None]
    weights = weight[None, :]
    big = (2 * half, width)
    small = (half, width)
    rule = (arity, tiles, width)
    window = (list_len, tiles, width)

    gathered = jnp.stack(
        [
            lax.dynamic_slice_in_dim(f.astype(jnp.float32), core * piece, piece, 0)
            for f in (atom_value, observed, target_value)
        ]
    )
    for bit in order:
        arrived = exchange(gathered, (bit, bit), count)
        high = (device // bit) % 2 == 1
        gathered = jnp.where(
            high,
            jnp.concatenate([arrived, gathered], axis=1),
            jnp.concatenate([gathered, arrived], axis=1),
        )
    gathered = jnp.concatenate([gathered, swap_cores(gathered)], axis=1)
    values, fixed, targets = gathered[0], gathered[1], gathered[2]

    def reduce_all(keep, send):
        mine = all_sum(keep + swap_cores(send), count)
        return mine, swap_cores(mine)

    count_keep, count_send = call(
        lambda *r: count_kernel(*r, list_len=list_len), (place, slots), 1, (small, small), (big,)
    )
    counted = jnp.concatenate(reduce_all(count_keep, count_send), axis=0)

    moved, keep, send = call(
        lambda *r: sweep_kernel(*r, list_len=list_len, first=True),
        (place, values, slots, coeffs, offsets, duals, templates, weights),
        1,
        (rule, small, small),
        (window, big),
    )
    mine, other = reduce_all(keep, send)
    moved, duals, values, keep, send = call(
        lambda *r: sweep_kernel(*r, list_len=list_len, first=False),
        (place, mine, other, values, counted, fixed,
         slots, coeffs, offsets, duals, moved, templates, weights),
        1,
        (rule, rule, big, small, small),
        (window, big),
    )
    mine, other = reduce_all(keep, send)
    (energy_target,) = call(
        lambda *r: energy_kernel(*r, list_len=list_len, last=False),
        (place, targets, slots, coeffs, offsets, templates, weights),
        1,
        ((1, TEMPL),),
        (window,),
    )
    energy_value, dual_next, consensus = call(
        lambda *r: energy_kernel(*r, list_len=list_len, last=True),
        (place, own, mine, other, values, counted, fixed,
         slots, coeffs, offsets, duals, moved, templates, weights),
        2,
        ((1, TEMPL), rule, (atom_blk, width)),
        (window, big),
    )
    energies = jnp.concatenate([energy_value, energy_target], axis=0)
    energies = all_sum(energies + swap_cores(energies), count)
    e_value, e_target = energies[0], energies[1]
    weight_next = weight * jnp.exp(-LEARN_RATE * (e_value - e_target) / (e_value + e_target + 1.0))
    return consensus, dual_next.reshape(dual_value.shape), weight_next


def solution(mesh):
    in_specs = (
        P("blk", None),
        P("blk", None),
        P("blk", None),
        P(),
        P(),
        P(None, "grp", "blk"),
        P(None, "grp", "blk"),
        P("grp", "blk"),
        P(None, "grp", "blk"),
        P("grp", "blk"),
        P(),
    )
    out_specs = (P("blk", None), P(None, "grp", "blk"), P())
    return jax.shard_map(local, mesh=mesh, in_specs=in_specs, out_specs=out_specs, check_vma=False)
```

```python
import jax
import jax.numpy as jnp
from jax import lax
from jax.experimental import pallas as pl
from jax.experimental.pallas import tpu as pltpu
from jax.sharding import PartitionSpec as P

TEMPL = 40
PENALTY = 1.0
LEARN_RATE = 2.0
GROUP = 8
LIMIT = 8 * 1024 * 1024
UNROLL = 8
VMEM = pltpu.VMEM
SMEM = pltpu.SMEM


def bits_of(count):
    bits, bit = [], 1
    while bit < count:
        bits.append(bit)
        bit *= 2
    return bits


def swap_cores(value):
    return lax.ppermute(value, "grp", [(0, 1), (1, 0)])


def exchange(value, steps, count):
    perm = [
        (2 * b + core, 2 * (b ^ steps[core]) + core) for b in range(count) for core in range(2)
    ]
    return lax.ppermute(value, ("blk", "grp"), perm)


def sum_steps(count, turned):
    bits = bits_of(count)
    middle = len(bits) // 2
    low, high = bits[:middle], bits[middle:]
    if turned:
        low, high = high, low
    return list(zip(low + high, low[::-1] + high[::-1]))


def all_sum(values, count):
    orders = [sum_steps(count, i % 2 == 1) for i in range(len(values))]
    for turn in range(len(orders[0])):
        sent = [exchange(v, order[turn], count) for v, order in zip(values, orders)]
        values = [v + r for v, r in zip(values, sent)]
    return values


def row_of(row, height, width):
    return jnp.broadcast_to(row, (height, width))


def refresh(total, before, counted, observed):
    moved = jnp.clip((total + before) / (counted + 1.0), 0.0, 1.0)
    return jnp.where(observed > 0.5, before, moved)


def load_windows(place_ref, field_ref, window_ref, tiles, list_len):
    @pl.loop(0, tiles // GROUP, unroll=UNROLL)
    def _(group):
        base = pl.multiple_of(group * GROUP, GROUP)
        for i in range(GROUP):
            for k in range(list_len):
                spot = place_ref[(base + i) * list_len + k]
                window_ref[k, pl.ds(base + i, 1), :] = field_ref[pl.ds(spot, 1), :]


def fetch_rows(window_ref, rows, slot, list_len, width):
    lane = slot & (width - 1)
    which = slot // width
    result = jnp.zeros(slot.shape, jnp.float32)
    for k in range(list_len):
        taken = jnp.take_along_axis(window_ref[k, rows, :], lane, axis=1, mode="promise_in_bounds")
        result = jnp.where(which == k, taken, result)
    return result


def split_three(value):
    first = value.astype(jnp.bfloat16).astype(jnp.float32)
    rest = value - first
    second = rest.astype(jnp.bfloat16).astype(jnp.float32)
    return first, second, rest - second


def scatter_tile(place_ref, sum_ref, tile, lows, tops, values, list_len, width):
    narrow = width // 2
    height = 2 * list_len
    row = lax.broadcasted_iota(jnp.int32, (height, width), 0)
    spot = lax.broadcasted_iota(jnp.int32, (narrow, width), 0)
    hot, left = [], []
    for low, top, parts in zip(lows, tops, values):
        hot.append((row_of(low, narrow, width) == spot).astype(jnp.float32).astype(jnp.bfloat16))
        here = row_of(top, height, width) == row
        left.append(
            jnp.concatenate(
                [jnp.where(here, row_of(part, height, width), 0.0) for part in parts], axis=0
            ).astype(jnp.bfloat16)
        )
    summed = lax.dot_general(
        jnp.concatenate(left, axis=1),
        jnp.concatenate(hot, axis=1),
        (((1,), (1,)), ((), ())),
        preferred_element_type=jnp.float32,
    )
    total = summed[:height]
    for j in range(1, len(values[0])):
        total = total + summed[j * height : (j + 1) * height]
    total = jnp.concatenate([total[:list_len], total[list_len:]], axis=1)
    spots = [place_ref[tile * list_len + k] for k in range(list_len)]
    olds = [sum_ref[pl.ds(at, 1), :] for at in spots]
    for k, at in enumerate(spots):
        sum_ref[pl.ds(at, 1), :] = olds[k] + total[k : k + 1]


def slot_parts(slot, list_len, width):
    narrow = width // 2
    low = slot & (narrow - 1)
    top = ((slot & (width - 1)) // narrow) * list_len + slot // width
    return low, jnp.where(slot < list_len * width, top, 2 * list_len)


def hand_out(sum_ref, refs):
    height = refs[0].shape[0]
    for i, ref in enumerate(refs):
        ref[...] = sum_ref[i * height : (i + 1) * height]


def renew(field_ref, source_refs, before_ref, counted_refs, observed_ref):
    height = source_refs[0].shape[0]
    share = counted_refs[0].shape[0] // height
    for i, source in enumerate(source_refs):
        part = slice(i * height, (i + 1) * height)
        counted = counted_refs[i // share][(i % share) * height : (i % share + 1) * height]
        field_ref[part] = refresh(source[...], before_ref[part], counted, observed_ref[part])


def count_kernel(*refs, list_len):
    place_ref, slot_ref = refs[:2]
    out_refs, sum_ref = refs[2:-1], refs[-1]
    arity, tiles, width = slot_ref.shape
    sum_ref[...] = jnp.zeros_like(sum_ref)

    @pl.loop(0, tiles // GROUP, unroll=UNROLL)
    def _(group):
        base = pl.multiple_of(group * GROUP, GROUP)
        rows = pl.ds(base, GROUP)
        halves = [slot_parts(slot_ref[s, rows, :], list_len, width) for s in range(arity)]
        one = jnp.ones((1, width), jnp.float32)
        for i in range(GROUP):
            scatter_tile(
                place_ref,
                sum_ref,
                base + i,
                [h[0][i : i + 1] for h in halves],
                [h[1][i : i + 1] for h in halves],
                [(one,)] * arity,
                list_len,
                width,
            )

    hand_out(sum_ref, out_refs)


def sweep_kernel(*refs, list_len, first, streams):
    refs = list(refs)

    def take(number):
        taken = refs[:number]
        del refs[:number]
        return taken

    (place_ref,) = take(1)
    if first:
        (field_ref,) = take(1)
    else:
        sources, counts = take(streams), take(2)
        before_ref, observed_ref, old_ref = take(3)
    slot_ref, coef_ref, off_ref, dual_ref, temp_ref, weight_ref, moved_ref = take(7)
    if not first:
        next_ref, field_ref = take(2)
    out_refs = take(streams)
    window_ref, sum_ref = refs
    arity, tiles, width = slot_ref.shape
    templates = weight_ref.shape[1]
    if not first:
        renew(field_ref, sources, before_ref, counts, observed_ref)
    load_windows(place_ref, field_ref, window_ref, tiles, list_len)
    sum_ref[...] = jnp.zeros_like(sum_ref)

    @pl.loop(0, tiles // GROUP, unroll=UNROLL)
    def _(group):
        base = pl.multiple_of(group * GROUP, GROUP)
        rows = pl.ds(base, GROUP)
        templ = temp_ref[rows, :]
        hot = row_of(templ, GROUP, templates) == lax.broadcasted_iota(
            jnp.int32, (GROUP, templates), 1
        )
        weight = jnp.sum(
            jnp.where(hot, row_of(weight_ref[...], GROUP, templates), 0.0), axis=1, keepdims=True
        )
        weight = jnp.broadcast_to(weight, (GROUP, width))
        squared = jnp.broadcast_to(templ % 2 == 1, (GROUP, width))
        slots = [slot_ref[s, rows, :] for s in range(arity)]
        used = [q < list_len * width for q in slots]
        acts = [jnp.where(used[s], coef_ref[s, rows, :], 0.0) for s in range(arity)]
        copies = [fetch_rows(window_ref, rows, q, list_len, width) for q in slots]
        duals = [dual_ref[s, rows, :] for s in range(arity)]
        if not first:
            duals = [
                d + jnp.where(m, old_ref[s, rows, :] - c, 0.0)
                for s, (d, m, c) in enumerate(zip(duals, used, copies))
            ]
            for s in range(arity):
                next_ref[s, rows, :] = duals[s]
        shifted = [c - d for c, d in zip(copies, duals)]
        linear = sum(a * v for a, v in zip(acts, shifted)) + off_ref[rows, :]
        norm = sum(a * a for a in acts)
        plain = jnp.clip(linear / norm, 0.0, weight / PENALTY)
        square = 2.0 * weight * jnp.maximum(linear, 0.0) / (PENALTY + 2.0 * weight * norm)
        chosen = jnp.where(squared, square, plain)
        parts = []
        for s in range(arity):
            moved = shifted[s] - chosen * acts[s]
            moved_ref[s, rows, :] = moved
            parts.append(split_three(jnp.where(used[s], moved + duals[s], 0.0)))
        halves = [slot_parts(q, list_len, width) for q in slots]
        for i in range(GROUP):
            scatter_tile(
                place_ref,
                sum_ref,
                base + i,
                [h[0][i : i + 1] for h in halves],
                [h[1][i : i + 1] for h in halves],
                [tuple(p[i : i + 1] for p in part) for part in parts],
                list_len,
                width,
            )

    hand_out(sum_ref, out_refs)


def energy_kernel(*refs, list_len, streams):
    refs = list(refs)

    def take(number):
        taken = refs[:number]
        del refs[:number]
        return taken

    place_ref, own_ref = take(2)
    sources, counts = take(streams), take(2)
    before_ref, observed_ref, target_ref, old_ref = take(4)
    slot_ref, coef_ref, off_ref, dual_ref, temp_ref, weight_ref = take(6)
    energy_ref, next_ref, owned_ref = take(3)
    window_ref, other_ref, field_ref = refs
    arity, tiles, width = slot_ref.shape
    templates = weight_ref.shape[1]
    renew(field_ref, sources, before_ref, counts, observed_ref)
    piece = owned_ref.shape[0] // 2
    for h in range(2):
        start = pl.multiple_of(own_ref[h], GROUP)
        owned_ref[h * piece : (h + 1) * piece] = field_ref[pl.ds(start, piece), :]
    load_windows(place_ref, field_ref, window_ref, tiles, list_len)
    load_windows(place_ref, target_ref, other_ref, tiles, list_len)

    def step(group, totals):
        base = pl.multiple_of(group * GROUP, GROUP)
        rows = pl.ds(base, GROUP)
        templ = temp_ref[rows, :]
        hot = row_of(templ, GROUP, templates) == lax.broadcasted_iota(
            jnp.int32, (GROUP, templates), 1
        )
        squared = jnp.broadcast_to(templ % 2 == 1, (GROUP, width))
        linears = [off_ref[rows, :]] * 2
        for s in range(arity):
            slot = slot_ref[s, rows, :]
            used = slot < list_len * width
            act = jnp.where(used, coef_ref[s, rows, :], 0.0)
            copies = [
                fetch_rows(ref, rows, slot, list_len, width) for ref in (window_ref, other_ref)
            ]
            linears = [line + act * copy for line, copy in zip(linears, copies)]
            next_ref[s, rows, :] = dual_ref[s, rows, :] + jnp.where(
                used, old_ref[s, rows, :] - copies[0], 0.0
            )
        results = []
        for total, line in zip(totals, linears):
            positive = jnp.maximum(line, 0.0)
            rule = jnp.where(squared, positive * positive, positive)
            tile = jnp.sum(rule, axis=1, keepdims=True)
            results.append(
                total + jnp.where(hot, jnp.broadcast_to(tile, (GROUP, templates)), 0.0)
            )
        return tuple(results)

    zero = jnp.zeros((GROUP, templates), jnp.float32)
    totals = lax.fori_loop(0, tiles // GROUP, step, (zero, zero), unroll=UNROLL)
    for i, total in enumerate(totals):
        energy_ref[i : i + 1, :] = jnp.sum(total, axis=0, keepdims=True)


def specs(count, scalars):
    return [pl.BlockSpec(memory_space=SMEM)] * scalars + [
        pl.BlockSpec(memory_space=VMEM)
    ] * (count - scalars)


def call(body, args, scalars, outs, scratch, work):
    shapes = tuple(jax.ShapeDtypeStruct(s, jnp.float32) for s in outs)
    return pl.pallas_call(
        body,
        out_shape=shapes,
        in_specs=specs(len(args), scalars),
        out_specs=tuple(specs(len(outs), 0)),
        scratch_shapes=[VMEM(s, jnp.float32) for s in scratch],
        compiler_params=pltpu.CompilerParams(vmem_limit_bytes=LIMIT),
        cost_estimate=pl.CostEstimate(flops=0, bytes_accessed=work, transcendentals=0),
    )(*args)


def local(
    atom_value,
    target_value,
    observed,
    block_owner,
    block_local,
    slot_index,
    coefficient,
    offset,
    dual_value,
    template,
    weight,
):
    device = lax.axis_index("blk")
    count = lax.axis_size("blk")
    core = lax.axis_index("grp")
    groups = lax.axis_size("grp")
    atom_blk, width = atom_value.shape
    tiles = template.shape[1]
    list_len = block_owner.shape[1]
    arity = slot_index.shape[0]
    piece = atom_blk // 2
    half = count * piece
    bits = bits_of(count)
    middle = len(bits) // 2
    low, high = bits[:middle], bits[middle:]
    orders = (high + low, high[::-1] + low[::-1])

    def position(owner, part):
        spots = [
            sum(((owner // bit) % 2) << j for j, bit in enumerate(order)) for order in orders
        ]
        return jnp.where(part == 0, spots[0], spots[1])

    def place_of(owner, spot):
        part = spot // piece
        return (part ^ core) * half + position(owner, part) * piece + spot % piece

    start = device * tiles
    place = place_of(
        lax.dynamic_slice_in_dim(block_owner, start, tiles, 0),
        lax.dynamic_slice_in_dim(block_local, start, tiles, 0),
    ).reshape(-1)
    own = place_of(device, jnp.arange(2, dtype=jnp.int32) * piece)
    slots = slot_index.reshape(arity, tiles, width)
    coeffs = coefficient.reshape(arity, tiles, width)
    offsets = offset.reshape(tiles, width)
    duals = dual_value.reshape(arity, tiles, width)
    templates = (core * (TEMPL // groups) + template[0])[:, None]
    weights = weight[None, :]
    big = (2 * half, width)
    stream = (half // 2, width)
    small = (half, width)
    streams = 4
    rule = (arity, tiles, width)
    window = (list_len, tiles, width)

    gathered = jnp.stack(
        [
            lax.dynamic_slice_in_dim(f.astype(jnp.float32), core * piece, piece, 0)
            for f in (atom_value, observed, target_value)
        ]
    )
    counts = None
    pending = sum_steps(count, False)
    for turn, steps in enumerate(zip(*orders)):
        arrived = exchange(gathered, steps, count)
        step = jnp.where(core == 0, steps[0], steps[1])
        upper = (device // step) % 2 == 1
        if turn == 0:
            counts = call(
                lambda *r: count_kernel(*r, list_len=list_len),
                (place, slots), 1, (small, small), (big,), 10_000_000,
            )
        elif turn == 1:
            counts = counts[0] + swap_cores(counts[1])
        else:
            counts = counts + exchange(counts, pending.pop(0), count)
        gathered = jnp.where(
            upper,
            jnp.concatenate([arrived, gathered], axis=1),
            jnp.concatenate([gathered, arrived], axis=1),
        )
        gathered, counts = lax.optimization_barrier((gathered, counts))
    gathered = jnp.concatenate([gathered, swap_cores(gathered)], axis=1)
    values, fixed, targets = gathered[0], gathered[1], gathered[2]
    for steps in pending:
        counts = counts + exchange(counts, steps, count)
    counts = [counts, swap_cores(counts)]

    def reduce_all(parts):
        mine = [keep + swap_cores(send) for keep, send in zip(parts[:2], parts[2:])]
        mine = all_sum(mine, count)
        return mine + [swap_cores(m) for m in mine]

    moved, *sums = call(
        lambda *r: sweep_kernel(*r, list_len=list_len, first=True, streams=streams),
        (place, values, slots, coeffs, offsets, duals, templates, weights),
        1,
        (rule,) + (stream,) * streams,
        (window, big),
        15_000_000,
    )
    sums = reduce_all(sums)
    moved, duals, values, *sums = call(
        lambda *r: sweep_kernel(*r, list_len=list_len, first=False, streams=streams),
        (place, *sums, *counts, values, fixed, moved,
         slots, coeffs, offsets, duals, templates, weights),
        1,
        (rule, rule, big) + (stream,) * streams,
        (window, big),
        15_000_000,
    )
    sums = reduce_all(sums)
    energies, dual_next, consensus = call(
        lambda *r: energy_kernel(*r, list_len=list_len, streams=streams),
        (place, own, *sums, *counts, values, fixed, targets, moved,
         slots, coeffs, offsets, duals, templates, weights),
        2,
        ((2, TEMPL), rule, (atom_blk, width)),
        (window, window, big),
        10_000_000,
    )
    (energies,) = all_sum([energies + swap_cores(energies)], count)
    e_value, e_target = energies[0], energies[1]
    weight_next = weight * jnp.exp(-LEARN_RATE * (e_value - e_target) / (e_value + e_target + 1.0))
    return consensus, dual_next.reshape(dual_value.shape), weight_next


def solution(mesh):
    in_specs = (
        P("blk", None),
        P("blk", None),
        P("blk", None),
        P(),
        P(),
        P(None, "grp", "blk"),
        P(None, "grp", "blk"),
        P("grp", "blk"),
        P(None, "grp", "blk"),
        P("grp", "blk"),
        P(),
    )
    out_specs = (P("blk", None), P(None, "grp", "blk"), P())
    return jax.shard_map(local, mesh=mesh, in_specs=in_specs, out_specs=out_specs, check_vma=False)
```

```python
import jax
import jax.numpy as jnp
from jax import lax
from jax.experimental import pallas as pl
from jax.experimental.pallas import tpu as pltpu
from jax.sharding import PartitionSpec as P

TEMPL = 40
PENALTY = 1.0
LEARN_RATE = 2.0
GROUP = 8
LIMIT = 8 * 1024 * 1024
UNROLL = 8
VMEM = pltpu.VMEM
SMEM = pltpu.SMEM


def swap_cores(value):
    return lax.ppermute(value, "grp", [(0, 1), (1, 0)])


def deal(parts, axes="blk"):
    return lax.all_to_all(parts, axes, 0, 0, tiled=True)


def tell(own, count, meanwhile=()):
    mine = deal(jnp.broadcast_to(own[None], (count,) + own.shape)).reshape(-1, own.shape[1])
    if meanwhile:
        mine, meanwhile = lax.optimization_barrier((mine, meanwhile))
    gathered = jnp.concatenate([mine, swap_cores(mine)], axis=0)
    return (gathered,) + meanwhile if meanwhile else gathered


def collect(keep, send, count):
    parts = keep + swap_cores(send)
    return jnp.sum(deal(parts.reshape((count, -1) + parts.shape[1:])), axis=0)


def row_of(row, height, width):
    return jnp.broadcast_to(row, (height, width))


def load_windows(place_ref, field_ref, window_ref, tiles, list_len, shift=0):
    @pl.loop(0, tiles // GROUP, unroll=UNROLL)
    def _(group):
        base = pl.multiple_of(group * GROUP, GROUP)
        for i in range(GROUP):
            for k in range(list_len):
                spot = place_ref[(base + i) * list_len + k] + shift
                window_ref[k, pl.ds(base + i, 1), :] = field_ref[pl.ds(spot, 1), :]


def fetch_rows(window_ref, rows, slot, list_len, width):
    lane = slot & (width - 1)
    which = slot // width
    result = jnp.zeros(slot.shape, jnp.float32)
    for k in range(list_len):
        taken = jnp.take_along_axis(window_ref[k, rows, :], lane, axis=1, mode="promise_in_bounds")
        result = jnp.where(which == k, taken, result)
    return result


def split_three(value):
    first = value.astype(jnp.bfloat16).astype(jnp.float32)
    rest = value - first
    second = rest.astype(jnp.bfloat16).astype(jnp.float32)
    return first, second, rest - second


def scatter_tile(place_ref, sum_ref, beside, tile, lows, tops, values, list_len, width):
    narrow = width // 2
    height = 2 * list_len
    row = lax.broadcasted_iota(jnp.int32, (height, width), 0)
    spot = lax.broadcasted_iota(jnp.int32, (narrow, width), 0)
    hot, left = [], []
    for low, top, parts in zip(lows, tops, values):
        hot.append((row_of(low, narrow, width) == spot).astype(jnp.float32).astype(jnp.bfloat16))
        here = row_of(top, height, width) == row
        left.append(
            jnp.concatenate(
                [jnp.where(here, row_of(part, height, width), 0.0) for part in parts], axis=0
            ).astype(jnp.bfloat16)
        )
    summed = lax.dot_general(
        jnp.concatenate(left, axis=1),
        jnp.concatenate(hot, axis=1),
        (((1,), (1,)), ((), ())),
        preferred_element_type=jnp.float32,
    )
    bands = [summed[j * height : (j + 1) * height] for j in range(len(values[0]))]
    spots = [place_ref[tile * list_len + k] for k in range(list_len)]
    totals = [(0, bands[0] + bands[1] + bands[2])]
    if beside:
        totals.append((beside, bands[3]))
    for shift, total in totals:
        total = jnp.concatenate([total[:list_len], total[list_len:]], axis=1)
        olds = [sum_ref[pl.ds(at + shift, 1), :] for at in spots]
        for k, at in enumerate(spots):
            sum_ref[pl.ds(at + shift, 1), :] = olds[k] + total[k : k + 1]


def slot_parts(slot, list_len, width):
    narrow = width // 2
    low = slot & (narrow - 1)
    top = ((slot & (width - 1)) // narrow) * list_len + slot // width
    return low, jnp.where(slot < list_len * width, top, 2 * list_len)


def sweep_kernel(*refs, list_len, beside):
    first = beside > 0
    if first:
        (place_ref, field_ref, slot_ref, coef_ref, off_ref, dual_ref, temp_ref, weight_ref,
         moved_ref, keep_ref, send_ref, sum_ref, window_ref) = refs
    else:
        (place_ref, field_ref, slot_ref, coef_ref, off_ref, dual_ref, temp_ref, weight_ref,
         old_ref, moved_ref, next_ref, keep_ref, send_ref, sum_ref, window_ref) = refs
    arity, tiles, width = slot_ref.shape
    templates = weight_ref.shape[1]
    load_windows(place_ref, field_ref, window_ref, tiles, list_len)
    sum_ref[...] = jnp.zeros_like(sum_ref)
    one = jnp.ones((GROUP, width), jnp.float32)

    @pl.loop(0, tiles // GROUP, unroll=UNROLL)
    def _(group):
        base = pl.multiple_of(group * GROUP, GROUP)
        rows = pl.ds(base, GROUP)
        templ = temp_ref[rows, :]
        hot = row_of(templ, GROUP, templates) == lax.broadcasted_iota(
            jnp.int32, (GROUP, templates), 1
        )
        weight = jnp.sum(
            jnp.where(hot, row_of(weight_ref[...], GROUP, templates), 0.0), axis=1, keepdims=True
        )
        weight = jnp.broadcast_to(weight, (GROUP, width))
        squared = jnp.broadcast_to(templ % 2 == 1, (GROUP, width))
        slots = [slot_ref[s, rows, :] for s in range(arity)]
        used = [q < list_len * width for q in slots]
        acts = [jnp.where(used[s], coef_ref[s, rows, :], 0.0) for s in range(arity)]
        copies = [fetch_rows(window_ref, rows, q, list_len, width) for q in slots]
        duals = [dual_ref[s, rows, :] for s in range(arity)]
        if not first:
            duals = [
                d + jnp.where(m, old_ref[s, rows, :] - c, 0.0)
                for s, (d, m, c) in enumerate(zip(duals, used, copies))
            ]
            for s in range(arity):
                next_ref[s, rows, :] = duals[s]
        shifted = [c - d for c, d in zip(copies, duals)]
        linear = sum(a * v for a, v in zip(acts, shifted)) + off_ref[rows, :]
        norm = sum(a * a for a in acts)
        plain = jnp.clip(linear / norm, 0.0, weight / PENALTY)
        square = 2.0 * weight * jnp.maximum(linear, 0.0) / (PENALTY + 2.0 * weight * norm)
        chosen = jnp.where(squared, square, plain)
        parts = []
        for s in range(arity):
            moved = shifted[s] - chosen * acts[s]
            moved_ref[s, rows, :] = moved
            pieces = split_three(jnp.where(used[s], moved + duals[s], 0.0))
            parts.append(pieces + (one,) if first else pieces)
        halves = [slot_parts(q, list_len, width) for q in slots]
        for i in range(GROUP):
            scatter_tile(
                place_ref,
                sum_ref,
                beside,
                base + i,
                [h[0][i : i + 1] for h in halves],
                [h[1][i : i + 1] for h in halves],
                [tuple(p[i : i + 1] for p in part) for part in parts],
                list_len,
                width,
            )

    half = keep_ref.shape[0]
    keep_ref[...] = sum_ref[:half]
    send_ref[...] = sum_ref[half:]


def energy_kernel(*refs, list_len, beside):
    (place_ref, first_ref, own_ref, field_ref, start_ref, slot_ref, coef_ref, off_ref, dual_ref,
     temp_ref, weight_ref, old_ref, energy_ref, next_ref, owned_ref, window_ref, other_ref) = refs
    arity, tiles, width = slot_ref.shape
    templates = weight_ref.shape[1]
    piece = owned_ref.shape[0] // 2
    for h in range(2):
        start = pl.multiple_of(own_ref[h], GROUP)
        owned_ref[h * piece : (h + 1) * piece] = field_ref[pl.ds(start, piece), :]
    load_windows(place_ref, field_ref, window_ref, tiles, list_len)
    load_windows(first_ref, start_ref, other_ref, tiles, list_len, beside)

    def step(group, totals):
        base = pl.multiple_of(group * GROUP, GROUP)
        rows = pl.ds(base, GROUP)
        templ = temp_ref[rows, :]
        hot = row_of(templ, GROUP, templates) == lax.broadcasted_iota(
            jnp.int32, (GROUP, templates), 1
        )
        squared = jnp.broadcast_to(templ % 2 == 1, (GROUP, width))
        lines = [off_ref[rows, :]] * 2
        for s in range(arity):
            slot = slot_ref[s, rows, :]
            used = slot < list_len * width
            act = jnp.where(used, coef_ref[s, rows, :], 0.0)
            copies = [
                fetch_rows(ref, rows, slot, list_len, width) for ref in (window_ref, other_ref)
            ]
            lines = [line + act * copy for line, copy in zip(lines, copies)]
            next_ref[s, rows, :] = dual_ref[s, rows, :] + jnp.where(
                used, old_ref[s, rows, :] - copies[0], 0.0
            )
        results = []
        for total, line in zip(totals, lines):
            positive = jnp.maximum(line, 0.0)
            rule = jnp.where(squared, positive * positive, positive)
            tile = jnp.sum(rule, axis=1, keepdims=True)
            results.append(
                total + jnp.where(hot, jnp.broadcast_to(tile, (GROUP, templates)), 0.0)
            )
        return tuple(results)

    zero = jnp.zeros((GROUP, templates), jnp.float32)
    totals = lax.fori_loop(0, tiles // GROUP, step, (zero, zero), unroll=UNROLL)
    energy_ref[...] = jnp.concatenate(
        [jnp.sum(total, axis=0, keepdims=True) for total in totals], axis=1
    )


def specs(count, scalars):
    return [pl.BlockSpec(memory_space=SMEM)] * scalars + [
        pl.BlockSpec(memory_space=VMEM)
    ] * (count - scalars)


def call(body, args, scalars, outs, scratch, work):
    shapes = tuple(jax.ShapeDtypeStruct(s, jnp.float32) for s in outs)
    return pl.pallas_call(
        body,
        out_shape=shapes,
        in_specs=specs(len(args), scalars),
        out_specs=tuple(specs(len(outs), 0)),
        scratch_shapes=[VMEM(s, jnp.float32) for s in scratch],
        compiler_params=pltpu.CompilerParams(vmem_limit_bytes=LIMIT),
        cost_estimate=pl.CostEstimate(flops=0, bytes_accessed=work, transcendentals=0),
    )(*args)


def local(
    atom_value,
    target_value,
    observed,
    block_owner,
    block_local,
    slot_index,
    coefficient,
    offset,
    dual_value,
    template,
    weight,
):
    device = lax.axis_index("blk")
    count = lax.axis_size("blk")
    core = lax.axis_index("grp")
    groups = lax.axis_size("grp")
    atom_blk, width = atom_value.shape
    tiles = template.shape[1]
    list_len = block_owner.shape[1]
    arity = slot_index.shape[0]
    devices = count * groups
    piece = atom_blk // groups
    half = count * piece
    start = device * tiles
    owner = lax.dynamic_slice_in_dim(block_owner, start, tiles, 0)
    spot = lax.dynamic_slice_in_dim(block_local, start, tiles, 0)

    def place_of(owner, spot, stride):
        part = spot // piece
        return (part ^ core) * (count * stride) + owner * stride + spot % piece

    place_first = place_of(owner, spot, 2 * piece).reshape(-1)
    place = place_of(owner, spot, piece).reshape(-1)
    own = place_of(device, jnp.arange(2, dtype=jnp.int32) * piece, piece)
    slots = slot_index.reshape(arity, tiles, width)
    coeffs = coefficient.reshape(arity, tiles, width)
    offsets = offset.reshape(tiles, width)
    duals = dual_value.reshape(arity, tiles, width)
    templates = (core * (TEMPL // groups) + template[0])[:, None]
    weights = weight[None, :]
    rule = (arity, tiles, width)
    window = (list_len, tiles, width)

    def share(field):
        return lax.dynamic_slice_in_dim(field, core * piece, piece, 0)

    mine, fixed = share(atom_value), share(observed)
    start_fields, *early = tell(
        jnp.concatenate([mine, share(target_value)], axis=0),
        count,
        (place_first, place, own, fixed, templates, slots, coeffs, offsets, duals),
    )
    place_first, place, own, fixed, templates, slots, coeffs, offsets, duals = early
    moved, keep, send = call(
        lambda *r: sweep_kernel(*r, list_len=list_len, beside=piece),
        (place_first, start_fields, slots, coeffs, offsets, duals, templates, weights),
        1,
        (rule, (2 * half, width), (2 * half, width)),
        ((4 * half, width), window),
        15_000_000,
    )
    sums = collect(keep, send, count)
    counted = sums[piece:] + 1.0

    def refresh(sums, before):
        stepped = jnp.clip((sums + before) / counted, 0.0, 1.0)
        return jnp.where(fixed == 1, before, stepped)

    mine = refresh(sums[:piece], mine)
    values = tell(mine, count)
    moved, duals, keep, send = call(
        lambda *r: sweep_kernel(*r, list_len=list_len, beside=0),
        (place, values, slots, coeffs, offsets, duals, templates, weights, moved),
        1,
        (rule, rule, (half, width), (half, width)),
        ((2 * half, width), window),
        15_000_000,
    )
    values = tell(refresh(collect(keep, send, count), mine), count)
    energies, dual_next, consensus = call(
        lambda *r: energy_kernel(*r, list_len=list_len, beside=piece),
        (place, place_first, own, values, start_fields, slots, coeffs, offsets, duals, templates,
         weights, moved),
        3,
        ((1, 2 * TEMPL), rule, (atom_blk, width)),
        (window, window),
        10_000_000,
    )
    energies = deal(jnp.broadcast_to(energies[None], (devices, 1, 2 * TEMPL)), ("blk", "grp"))
    energies = jnp.sum(energies, axis=(0, 1))
    e_value, e_target = energies[:TEMPL], energies[TEMPL:]
    weight_next = weight * jnp.exp(-LEARN_RATE * (e_value - e_target) / (e_value + e_target + 1.0))
    return consensus, dual_next.reshape(dual_value.shape), weight_next


def solution(mesh):
    in_specs = (
        P("blk", None),
        P("blk", None),
        P("blk", None),
        P(),
        P(),
        P(None, "grp", "blk"),
        P(None, "grp", "blk"),
        P("grp", "blk"),
        P(None, "grp", "blk"),
        P("grp", "blk"),
        P(),
    )
    out_specs = (P("blk", None), P(None, "grp", "blk"), P())
    return jax.shard_map(local, mesh=mesh, in_specs=in_specs, out_specs=out_specs, check_vma=False)
```

```python
import jax
import jax.numpy as jnp
from jax import lax
from jax.experimental import pallas as pl
from jax.experimental.pallas import tpu as pltpu
from jax.sharding import PartitionSpec as P

TEMPL = 40
PENALTY = 1.0
LEARN_RATE = 2.0
GROUP = 8
LIMIT = 8 * 1024 * 1024
UNROLL = 8
VMEM = pltpu.VMEM
SMEM = pltpu.SMEM


def swap_cores(value):
    return lax.ppermute(value, "grp", [(0, 1), (1, 0)])


def deal(parts):
    return lax.all_to_all(parts, ("blk", "grp"), 0, 0, tiled=True)


def tell(own, meanwhile=()):
    mine = deal(own).reshape(-1, own.shape[-1])
    if meanwhile:
        mine, meanwhile = lax.optimization_barrier((mine, meanwhile))
    gathered = jnp.concatenate([mine, swap_cores(mine)], axis=0)
    return (gathered,) + meanwhile if meanwhile else gathered


def collect(keep, send, count):
    parts = keep + swap_cores(send)
    width = parts.shape[1]
    return jnp.sum(deal(parts.reshape(2 * count, -1, width)).reshape(count, -1, width), axis=0)


def row_of(row, height, width):
    return jnp.broadcast_to(row, (height, width))


def load_windows(place_ref, field_ref, windows, tiles, list_len):
    @pl.loop(0, tiles // GROUP, unroll=UNROLL)
    def _(group):
        base = pl.multiple_of(group * GROUP, GROUP)
        for i in range(GROUP):
            for k in range(list_len):
                spot = place_ref[(base + i) * list_len + k]
                for shift, window_ref in windows:
                    window_ref[k, pl.ds(base + i, 1), :] = field_ref[pl.ds(spot + shift, 1), :]


def fetch_rows(window_ref, rows, slot, list_len, width):
    lane = slot & (width - 1)
    which = slot // width
    result = jnp.zeros(slot.shape, jnp.float32)
    for k in range(list_len):
        taken = jnp.take_along_axis(window_ref[k, rows, :], lane, axis=1, mode="promise_in_bounds")
        result = jnp.where(which == k, taken, result)
    return result


def split_three(value):
    first = value.astype(jnp.bfloat16).astype(jnp.float32)
    rest = value - first
    second = rest.astype(jnp.bfloat16).astype(jnp.float32)
    return first, second, rest - second


def scatter_tile(place_ref, sum_ref, beside, tile, lows, tops, values, list_len, width):
    narrow = width // 2
    height = 2 * list_len
    row = lax.broadcasted_iota(jnp.int32, (height, width), 0)
    spot = lax.broadcasted_iota(jnp.int32, (narrow, width), 0)
    hot, left = [], []
    for low, top, parts in zip(lows, tops, values):
        hot.append((row_of(low, narrow, width) == spot).astype(jnp.float32).astype(jnp.bfloat16))
        here = row_of(top, height, width) == row
        left.append(
            jnp.concatenate(
                [jnp.where(here, row_of(part, height, width), 0.0) for part in parts], axis=0
            ).astype(jnp.bfloat16)
        )
    summed = lax.dot_general(
        jnp.concatenate(left, axis=1),
        jnp.concatenate(hot, axis=1),
        (((1,), (1,)), ((), ())),
        preferred_element_type=jnp.float32,
    )
    bands = [summed[j * height : (j + 1) * height] for j in range(len(values[0]))]
    spots = [place_ref[tile * list_len + k] for k in range(list_len)]
    totals = [(0, bands[0] + bands[1] + bands[2])]
    if beside:
        totals.append((beside, bands[3]))
    for shift, total in totals:
        total = jnp.concatenate([total[:list_len], total[list_len:]], axis=1)
        olds = [sum_ref[pl.ds(at + shift, 1), :] for at in spots]
        for k, at in enumerate(spots):
            sum_ref[pl.ds(at + shift, 1), :] = olds[k] + total[k : k + 1]


def slot_parts(slot, list_len, width):
    narrow = width // 2
    low = slot & (narrow - 1)
    top = ((slot & (width - 1)) // narrow) * list_len + slot // width
    return low, jnp.where(slot < list_len * width, top, 2 * list_len)


def rule_energy(line, squared, hot):
    positive = jnp.maximum(line, 0.0)
    rule = jnp.where(squared, positive * positive, positive)
    tile = jnp.sum(rule, axis=1, keepdims=True)
    return jnp.where(hot, jnp.broadcast_to(tile, hot.shape), 0.0)


def sweep_kernel(*refs, list_len, beside):
    first = beside > 0
    if first:
        (place_ref, field_ref, slot_ref, coef_ref, off_ref, dual_ref, temp_ref, weight_ref,
         moved_ref, energy_ref, keep_ref, send_ref, sum_ref, window_ref, other_ref) = refs
        windows = [(0, window_ref), (beside, other_ref)]
    else:
        (place_ref, field_ref, slot_ref, coef_ref, off_ref, dual_ref, temp_ref, weight_ref,
         old_ref, moved_ref, next_ref, keep_ref, send_ref, sum_ref, window_ref) = refs
        windows = [(0, window_ref)]
    arity, tiles, width = slot_ref.shape
    templates = weight_ref.shape[1]
    load_windows(place_ref, field_ref, windows, tiles, list_len)
    sum_ref[...] = jnp.zeros_like(sum_ref)
    one = jnp.ones((GROUP, width), jnp.float32)

    def step(group, energy):
        base = pl.multiple_of(group * GROUP, GROUP)
        rows = pl.ds(base, GROUP)
        templ = temp_ref[rows, :]
        hot = row_of(templ, GROUP, templates) == lax.broadcasted_iota(
            jnp.int32, (GROUP, templates), 1
        )
        weight = jnp.sum(
            jnp.where(hot, row_of(weight_ref[...], GROUP, templates), 0.0), axis=1, keepdims=True
        )
        weight = jnp.broadcast_to(weight, (GROUP, width))
        squared = jnp.broadcast_to(templ % 2 == 1, (GROUP, width))
        slots = [slot_ref[s, rows, :] for s in range(arity)]
        used = [q < list_len * width for q in slots]
        acts = [jnp.where(used[s], coef_ref[s, rows, :], 0.0) for s in range(arity)]
        if first:
            goals = [fetch_rows(other_ref, rows, q, list_len, width) for q in slots]
            line = sum(a * c for a, c in zip(acts, goals)) + off_ref[rows, :]
            energy = energy + rule_energy(line, squared, hot)
        copies = [fetch_rows(window_ref, rows, q, list_len, width) for q in slots]
        duals = [dual_ref[s, rows, :] for s in range(arity)]
        if not first:
            duals = [
                d + jnp.where(m, old_ref[s, rows, :] - c, 0.0)
                for s, (d, m, c) in enumerate(zip(duals, used, copies))
            ]
            for s in range(arity):
                next_ref[s, rows, :] = duals[s]
        shifted = [c - d for c, d in zip(copies, duals)]
        linear = sum(a * v for a, v in zip(acts, shifted)) + off_ref[rows, :]
        norm = sum(a * a for a in acts)
        plain = jnp.clip(linear / norm, 0.0, weight / PENALTY)
        square = 2.0 * weight * jnp.maximum(linear, 0.0) / (PENALTY + 2.0 * weight * norm)
        chosen = jnp.where(squared, square, plain)
        parts = []
        for s in range(arity):
            moved = shifted[s] - chosen * acts[s]
            moved_ref[s, rows, :] = moved
            pieces = split_three(jnp.where(used[s], moved + duals[s], 0.0))
            parts.append(pieces + (one,) if first else pieces)
        halves = [slot_parts(q, list_len, width) for q in slots]
        for i in range(GROUP):
            scatter_tile(
                place_ref,
                sum_ref,
                beside,
                base + i,
                [h[0][i : i + 1] for h in halves],
                [h[1][i : i + 1] for h in halves],
                [tuple(p[i : i + 1] for p in part) for part in parts],
                list_len,
                width,
            )
        return energy

    energy = jnp.zeros((GROUP, templates), jnp.float32)
    energy = lax.fori_loop(0, tiles // GROUP, step, energy, unroll=UNROLL)
    if first:
        energy_ref[...] = jnp.sum(energy, axis=0, keepdims=True)
    half = keep_ref.shape[0]
    keep_ref[...] = sum_ref[:half]
    send_ref[...] = sum_ref[half:]


def energy_kernel(*refs, list_len):
    (place_ref, own_ref, field_ref, slot_ref, coef_ref, off_ref, dual_ref, temp_ref, goal_ref,
     old_ref, energy_ref, next_ref, owned_ref, window_ref) = refs
    arity, tiles, width = slot_ref.shape
    templates = goal_ref.shape[1]
    piece = owned_ref.shape[0] // own_ref.shape[0]
    for h in range(own_ref.shape[0]):
        start = pl.multiple_of(own_ref[h], GROUP)
        owned_ref[h * piece : (h + 1) * piece] = field_ref[pl.ds(start, piece), :]
    load_windows(place_ref, field_ref, [(0, window_ref)], tiles, list_len)

    def step(group, energy):
        base = pl.multiple_of(group * GROUP, GROUP)
        rows = pl.ds(base, GROUP)
        templ = temp_ref[rows, :]
        hot = row_of(templ, GROUP, templates) == lax.broadcasted_iota(
            jnp.int32, (GROUP, templates), 1
        )
        squared = jnp.broadcast_to(templ % 2 == 1, (GROUP, width))
        line = off_ref[rows, :]
        for s in range(arity):
            slot = slot_ref[s, rows, :]
            used = slot < list_len * width
            copy = fetch_rows(window_ref, rows, slot, list_len, width)
            line = line + jnp.where(used, coef_ref[s, rows, :], 0.0) * copy
            next_ref[s, rows, :] = dual_ref[s, rows, :] + jnp.where(
                used, old_ref[s, rows, :] - copy, 0.0
            )
        return energy + rule_energy(line, squared, hot)

    energy = jnp.zeros((GROUP, templates), jnp.float32)
    energy = lax.fori_loop(0, tiles // GROUP, step, energy, unroll=UNROLL)
    energy_ref[...] = jnp.concatenate(
        [jnp.sum(energy, axis=0, keepdims=True), goal_ref[...]], axis=1
    )


def specs(count, scalars):
    return [pl.BlockSpec(memory_space=SMEM)] * scalars + [
        pl.BlockSpec(memory_space=VMEM)
    ] * (count - scalars)


def call(body, args, scalars, outs, scratch, work):
    shapes = tuple(jax.ShapeDtypeStruct(s, jnp.float32) for s in outs)
    return pl.pallas_call(
        body,
        out_shape=shapes,
        in_specs=specs(len(args), scalars),
        out_specs=tuple(specs(len(outs), 0)),
        scratch_shapes=[VMEM(s, jnp.float32) for s in scratch],
        compiler_params=pltpu.CompilerParams(vmem_limit_bytes=LIMIT),
        cost_estimate=pl.CostEstimate(flops=0, bytes_accessed=work, transcendentals=0),
    )(*args)


def local(
    atom_value,
    target_value,
    observed,
    block_owner,
    block_local,
    slot_index,
    coefficient,
    offset,
    dual_value,
    template,
    weight,
):
    device = lax.axis_index("blk")
    count = lax.axis_size("blk")
    core = lax.axis_index("grp")
    groups = lax.axis_size("grp")
    atom_blk, width = atom_value.shape
    tiles = template.shape[1]
    list_len = block_owner.shape[1]
    arity = slot_index.shape[0]
    devices = count * groups
    piece = atom_blk // groups
    part = piece // 2
    half = devices * part
    start = device * tiles
    owner = lax.dynamic_slice_in_dim(block_owner, start, tiles, 0)
    spot = lax.dynamic_slice_in_dim(block_local, start, tiles, 0)

    def place_of(owner, spot, stride):
        holder = owner * groups + spot // piece
        handler = (spot // part) % 2
        return (handler ^ core) * (devices * stride) + holder * stride + spot % part

    place_first = place_of(owner, spot, piece).reshape(-1)
    place = place_of(owner, spot, part).reshape(-1)
    own = place_of(device, jnp.arange(2 * groups, dtype=jnp.int32) * part, part)
    slots = slot_index.reshape(arity, tiles, width)
    coeffs = coefficient.reshape(arity, tiles, width)
    offsets = offset.reshape(tiles, width)
    duals = dual_value.reshape(arity, tiles, width)
    templates = (core * (TEMPL // groups) + template[0])[:, None]
    weights = weight[None, :]
    rule = (arity, tiles, width)
    window = (list_len, tiles, width)

    def share(field):
        return lax.dynamic_slice_in_dim(field, core * piece, piece, 0)

    def spread(field):
        return jnp.broadcast_to(
            field.reshape(1, 2, part, width), (count, 2, part, width)
        ).reshape(devices, part, width)

    start_fields, *early = tell(
        jnp.concatenate([spread(share(atom_value)), spread(share(target_value))], axis=1),
        (place_first, place, own, share(atom_value), share(observed), templates, slots, coeffs,
         offsets, duals, weights),
    )
    (place_first, place, own, mine, fixed, templates, slots, coeffs, offsets, duals,
     weights) = early
    moved, e_target, keep, send = call(
        lambda *r: sweep_kernel(*r, list_len=list_len, beside=part),
        (place_first, start_fields, slots, coeffs, offsets, duals, templates, weights),
        1,
        (rule, (1, TEMPL), (2 * half, width), (2 * half, width)),
        ((4 * half, width), window, window),
        15_000_000,
    )
    sums = collect(keep, send, count)
    sums = sums.reshape(2, 2, part, width)
    counted = sums[:, 1].reshape(piece, width) + 1.0

    def refresh(sums, before):
        stepped = jnp.clip((sums + before) / counted, 0.0, 1.0)
        return jnp.where(fixed == 1, before, stepped)

    mine = refresh(sums[:, 0].reshape(piece, width), mine)
    values = tell(spread(mine))
    moved, duals, keep, send = call(
        lambda *r: sweep_kernel(*r, list_len=list_len, beside=0),
        (place, values, slots, coeffs, offsets, duals, templates, weights, moved),
        1,
        (rule, rule, (half, width), (half, width)),
        ((2 * half, width), window),
        15_000_000,
    )
    values = tell(spread(refresh(collect(keep, send, count), mine)))
    energies, dual_next, consensus = call(
        lambda *r: energy_kernel(*r, list_len=list_len),
        (place, own, values, slots, coeffs, offsets, duals, templates, e_target, moved),
        2,
        ((1, 2 * TEMPL), rule, (atom_blk, width)),
        (window,),
        10_000_000,
    )
    energies = deal(jnp.broadcast_to(energies[None], (devices, 1, 2 * TEMPL)))
    energies = jnp.sum(energies, axis=(0, 1))
    e_value, e_target = energies[:TEMPL], energies[TEMPL:]
    weight_next = weight * jnp.exp(-LEARN_RATE * (e_value - e_target) / (e_value + e_target + 1.0))
    return consensus, dual_next.reshape(dual_value.shape), weight_next


def solution(mesh):
    in_specs = (
        P("blk", None),
        P("blk", None),
        P("blk", None),
        P(),
        P(),
        P(None, "grp", "blk"),
        P(None, "grp", "blk"),
        P("grp", "blk"),
        P(None, "grp", "blk"),
        P("grp", "blk"),
        P(),
    )
    out_specs = (P("blk", None), P(None, "grp", "blk"), P())
    return jax.shard_map(local, mesh=mesh, in_specs=in_specs, out_specs=out_specs, check_vma=False)
```

```python
import jax
import jax.numpy as jnp
from jax import lax
from jax.experimental import pallas as pl
from jax.experimental.pallas import tpu as pltpu
from jax.sharding import PartitionSpec as P

TEMPL = 40
PENALTY = 1.0
LEARN_RATE = 2.0
GROUP = 8
LIMIT = 8 * 1024 * 1024
UNROLL = 8
VMEM = pltpu.VMEM
SMEM = pltpu.SMEM


def swap_cores(value):
    return lax.ppermute(value, "grp", [(0, 1), (1, 0)])


def deal(parts):
    return lax.all_to_all(parts, ("blk", "grp"), 0, 0, tiled=True)


def tell(own, meanwhile=()):
    mine = deal(own).reshape(-1, own.shape[-1])
    if meanwhile:
        mine, meanwhile = lax.optimization_barrier((mine, meanwhile))
    gathered = jnp.concatenate([mine, swap_cores(mine)], axis=0)
    return (gathered,) + meanwhile if meanwhile else gathered


def collect(parts, count):
    return jnp.sum(deal(parts).reshape(count, -1, parts.shape[-1]), axis=0)


def row_of(row, height, width):
    return jnp.broadcast_to(row, (height, width))


def load_windows(place_ref, field_ref, windows, tiles, list_len):
    @pl.loop(0, tiles // GROUP, unroll=UNROLL)
    def _(group):
        base = pl.multiple_of(group * GROUP, GROUP)
        for i in range(GROUP):
            for k in range(list_len):
                spot = place_ref[(base + i) * list_len + k]
                for shift, window_ref in windows:
                    window_ref[k, pl.ds(base + i, 1), :] = field_ref[pl.ds(spot + shift, 1), :]


def fetch_rows(window_ref, rows, slot, list_len, width):
    lane = slot & (width - 1)
    which = slot // width
    result = jnp.zeros(slot.shape, jnp.float32)
    for k in range(list_len):
        taken = jnp.take_along_axis(window_ref[k, rows, :], lane, axis=1, mode="promise_in_bounds")
        result = jnp.where(which == k, taken, result)
    return result


def split_three(value):
    first = value.astype(jnp.bfloat16).astype(jnp.float32)
    rest = value - first
    second = rest.astype(jnp.bfloat16).astype(jnp.float32)
    return first, second, rest - second


def one_hot(low, narrow, width):
    packed = jnp.broadcast_to(low.astype(jnp.float32), (16, width)).astype(jnp.bfloat16)
    spot = lax.broadcasted_iota(jnp.int32, (narrow, width), 0)
    spot = spot.astype(jnp.float32).astype(jnp.bfloat16)
    same = jnp.concatenate([packed] * (narrow // 16), axis=0) == spot
    return jnp.where(same, jnp.bfloat16(1), jnp.bfloat16(0))


def product(left, hot):
    return lax.dot_general(
        left, hot, (((1,), (1,)), ((), ())), preferred_element_type=jnp.float32
    )


def scatter_pair(place_ref, sum_ref, tile, lows, tops, values, list_len, width):
    narrow = width // 2
    height = 2 * list_len
    pieces = len(values[0][0])
    bands = pieces + pieces % 2
    row = lax.broadcasted_iota(jnp.int32, (height, width), 0)
    blank = jnp.zeros((height, width), jnp.float32)
    empty = jnp.zeros((bands * height, width), jnp.bfloat16)
    hots, lefts = [], []
    for own_lows, own_tops, own_values in zip(lows, tops, values):
        hots.append([one_hot(low, narrow, width) for low in own_lows])
        left = []
        for top, parts in zip(own_tops, own_values):
            here = row_of(top, height, width) == row
            rows = [jnp.where(here, row_of(part, height, width), 0.0) for part in parts]
            rows = rows + [blank] * (bands - len(rows))
            left.append(jnp.concatenate(rows, axis=0).astype(jnp.bfloat16))
        lefts.append(left)
    shared = product(
        jnp.concatenate(
            [
                jnp.concatenate([lefts[0][-1], empty], axis=1),
                jnp.concatenate([empty, lefts[1][-1]], axis=1),
            ],
            axis=0,
        ),
        jnp.concatenate([hots[0][-1], hots[1][-1]], axis=1),
    )
    for j in range(2):
        summed = shared[j * bands * height : (j + 1) * bands * height]
        summed = summed + product(
            jnp.concatenate(lefts[j][:-1], axis=1), jnp.concatenate(hots[j][:-1], axis=1)
        )
        parts = [summed[i * height : (i + 1) * height] for i in range(bands)]
        spots = [place_ref[(tile + j) * list_len + k] for k in range(list_len)]
        total = sum(parts[1:pieces], parts[0])
        total = jnp.concatenate([total[:list_len], total[list_len:]], axis=1)
        olds = [sum_ref[pl.ds(at, 1), :] for at in spots]
        for k, at in enumerate(spots):
            sum_ref[pl.ds(at, 1), :] = olds[k] + total[k : k + 1]


def slot_parts(slot, list_len, width):
    narrow = width // 2
    low = slot & (narrow - 1)
    top = ((slot & (width - 1)) // narrow) * list_len + slot // width
    return low, jnp.where(slot < list_len * width, top, 2 * list_len)


def count_kernel(place_ref, slot_ref, keep_ref, send_ref, sum_ref, *, list_len):
    arity, tiles, width = slot_ref.shape
    sum_ref[...] = jnp.zeros_like(sum_ref)
    one = (jnp.ones((1, width), jnp.float32),)

    @pl.loop(0, tiles // GROUP, unroll=UNROLL)
    def _(group):
        base = pl.multiple_of(group * GROUP, GROUP)
        rows = pl.ds(base, GROUP)
        halves = [slot_parts(slot_ref[s, rows, :], list_len, width) for s in range(arity)]
        for i in range(0, GROUP, 2):
            pair = (slice(i, i + 1), slice(i + 1, i + 2))
            scatter_pair(
                place_ref,
                sum_ref,
                base + i,
                [[h[0][at] for h in halves] for at in pair],
                [[h[1][at] for h in halves] for at in pair],
                [[one] * arity for at in pair],
                list_len,
                width,
            )

    half = keep_ref.shape[0]
    keep_ref[...] = sum_ref[:half]
    send_ref[...] = sum_ref[half:]


def rule_energy(line, squared, hot):
    positive = jnp.maximum(line, 0.0)
    rule = jnp.where(squared, positive * positive, positive)
    tile = jnp.sum(rule, axis=1, keepdims=True)
    return jnp.where(hot, jnp.broadcast_to(tile, hot.shape), 0.0)


def sweep_kernel(*refs, list_len, beside):
    first = beside > 0
    if first:
        (place_ref, first_ref, field_ref, slot_ref, coef_ref, off_ref, dual_ref, temp_ref,
         weight_ref, moved_ref, energy_ref, keep_ref, send_ref, sum_ref, window_ref, other_ref) = refs
        windows = [(0, window_ref), (beside, other_ref)]
    else:
        (place_ref, field_ref, slot_ref, coef_ref, off_ref, dual_ref, temp_ref, weight_ref,
         old_ref, moved_ref, next_ref, keep_ref, send_ref, sum_ref, window_ref) = refs
        first_ref, windows = place_ref, [(0, window_ref)]
    arity, tiles, width = slot_ref.shape
    templates = weight_ref.shape[1]
    load_windows(first_ref, field_ref, windows, tiles, list_len)
    sum_ref[...] = jnp.zeros_like(sum_ref)

    def step(group, energy):
        base = pl.multiple_of(group * GROUP, GROUP)
        rows = pl.ds(base, GROUP)
        templ = temp_ref[rows, :]
        hot = row_of(templ, GROUP, templates) == lax.broadcasted_iota(
            jnp.int32, (GROUP, templates), 1
        )
        weight = jnp.sum(
            jnp.where(hot, row_of(weight_ref[...], GROUP, templates), 0.0), axis=1, keepdims=True
        )
        weight = jnp.broadcast_to(weight, (GROUP, width))
        squared = jnp.broadcast_to(templ % 2 == 1, (GROUP, width))
        slots = [slot_ref[s, rows, :] for s in range(arity)]
        used = [q < list_len * width for q in slots]
        acts = [jnp.where(used[s], coef_ref[s, rows, :], 0.0) for s in range(arity)]
        if first:
            goals = [fetch_rows(other_ref, rows, q, list_len, width) for q in slots]
            line = sum(a * c for a, c in zip(acts, goals)) + off_ref[rows, :]
            energy = energy + rule_energy(line, squared, hot)
        copies = [fetch_rows(window_ref, rows, q, list_len, width) for q in slots]
        duals = [dual_ref[s, rows, :] for s in range(arity)]
        if not first:
            duals = [
                d + jnp.where(m, old_ref[s, rows, :] - c, 0.0)
                for s, (d, m, c) in enumerate(zip(duals, used, copies))
            ]
            for s in range(arity):
                next_ref[s, rows, :] = duals[s]
        shifted = [c - d for c, d in zip(copies, duals)]
        linear = sum(a * v for a, v in zip(acts, shifted)) + off_ref[rows, :]
        norm = sum(a * a for a in acts)
        plain = jnp.clip(linear / norm, 0.0, weight / PENALTY)
        square = 2.0 * weight * jnp.maximum(linear, 0.0) / (PENALTY + 2.0 * weight * norm)
        chosen = jnp.where(squared, square, plain)
        parts = []
        for s in range(arity):
            moved = shifted[s] - chosen * acts[s]
            moved_ref[s, rows, :] = moved
            parts.append(split_three(jnp.where(used[s], moved + duals[s], 0.0)))
        halves = [slot_parts(q, list_len, width) for q in slots]
        for i in range(0, GROUP, 2):
            pair = (slice(i, i + 1), slice(i + 1, i + 2))
            scatter_pair(
                place_ref,
                sum_ref,
                base + i,
                [[h[0][at] for h in halves] for at in pair],
                [[h[1][at] for h in halves] for at in pair],
                [[tuple(p[at] for p in part) for part in parts] for at in pair],
                list_len,
                width,
            )
        return energy

    energy = jnp.zeros((GROUP, templates), jnp.float32)
    energy = lax.fori_loop(0, tiles // GROUP, step, energy, unroll=UNROLL)
    if first:
        energy_ref[...] = jnp.sum(energy, axis=0, keepdims=True)
    half = keep_ref.shape[0]
    keep_ref[...] = sum_ref[:half]
    send_ref[...] = sum_ref[half:]


def energy_kernel(*refs, list_len):
    (place_ref, own_ref, field_ref, slot_ref, coef_ref, off_ref, dual_ref, temp_ref, goal_ref,
     old_ref, energy_ref, next_ref, owned_ref, window_ref) = refs
    arity, tiles, width = slot_ref.shape
    templates = goal_ref.shape[1]
    piece = owned_ref.shape[0] // own_ref.shape[0]
    for h in range(own_ref.shape[0]):
        start = pl.multiple_of(own_ref[h], GROUP)
        owned_ref[h * piece : (h + 1) * piece] = field_ref[pl.ds(start, piece), :]
    load_windows(place_ref, field_ref, [(0, window_ref)], tiles, list_len)

    def step(group, energy):
        base = pl.multiple_of(group * GROUP, GROUP)
        rows = pl.ds(base, GROUP)
        templ = temp_ref[rows, :]
        hot = row_of(templ, GROUP, templates) == lax.broadcasted_iota(
            jnp.int32, (GROUP, templates), 1
        )
        squared = jnp.broadcast_to(templ % 2 == 1, (GROUP, width))
        line = off_ref[rows, :]
        for s in range(arity):
            slot = slot_ref[s, rows, :]
            used = slot < list_len * width
            copy = fetch_rows(window_ref, rows, slot, list_len, width)
            line = line + jnp.where(used, coef_ref[s, rows, :], 0.0) * copy
            next_ref[s, rows, :] = dual_ref[s, rows, :] + jnp.where(
                used, old_ref[s, rows, :] - copy, 0.0
            )
        return energy + rule_energy(line, squared, hot)

    energy = jnp.zeros((GROUP, templates), jnp.float32)
    energy = lax.fori_loop(0, tiles // GROUP, step, energy, unroll=UNROLL)
    energy_ref[...] = jnp.concatenate(
        [jnp.sum(energy, axis=0, keepdims=True), goal_ref[...]], axis=1
    )


def specs(count, scalars):
    return [pl.BlockSpec(memory_space=SMEM)] * scalars + [
        pl.BlockSpec(memory_space=VMEM)
    ] * (count - scalars)


def call(body, args, scalars, outs, scratch, work):
    shapes = tuple(jax.ShapeDtypeStruct(s, jnp.float32) for s in outs)
    return pl.pallas_call(
        body,
        out_shape=shapes,
        in_specs=specs(len(args), scalars),
        out_specs=tuple(specs(len(outs), 0)),
        scratch_shapes=[VMEM(s, jnp.float32) for s in scratch],
        compiler_params=pltpu.CompilerParams(vmem_limit_bytes=LIMIT),
        cost_estimate=pl.CostEstimate(flops=0, bytes_accessed=work, transcendentals=0),
    )(*args)


def local(
    atom_value,
    target_value,
    observed,
    block_owner,
    block_local,
    slot_index,
    coefficient,
    offset,
    dual_value,
    template,
    weight,
):
    device = lax.axis_index("blk")
    count = lax.axis_size("blk")
    core = lax.axis_index("grp")
    groups = lax.axis_size("grp")
    atom_blk, width = atom_value.shape
    tiles = template.shape[1]
    list_len = block_owner.shape[1]
    arity = slot_index.shape[0]
    devices = count * groups
    piece = atom_blk // groups
    part = piece // 2
    half = devices * part
    start = device * tiles
    owner = lax.dynamic_slice_in_dim(block_owner, start, tiles, 0)
    spot = lax.dynamic_slice_in_dim(block_local, start, tiles, 0)

    def place_of(owner, spot, stride):
        holder = owner * groups + spot // piece
        handler = (spot // part) % 2
        return (handler ^ core) * (devices * stride) + holder * stride + spot % part

    place_first = place_of(owner, spot, piece).reshape(-1)
    place = place_of(owner, spot, part).reshape(-1)
    own = place_of(device, jnp.arange(2 * groups, dtype=jnp.int32) * part, part)
    slots = slot_index.reshape(arity, tiles, width)
    coeffs = coefficient.reshape(arity, tiles, width)
    offsets = offset.reshape(tiles, width)
    duals = dual_value.reshape(arity, tiles, width)
    templates = (core * (TEMPL // groups) + template[0])[:, None]
    weights = weight[None, :]
    rule = (arity, tiles, width)
    window = (list_len, tiles, width)

    def share(field):
        return lax.dynamic_slice_in_dim(field, core * piece, piece, 0)

    def spread(field):
        return jnp.broadcast_to(
            field.reshape(1, 2, part, width), (count, 2, part, width)
        ).reshape(devices, part, width)

    def by_device(keep, send):
        return (keep + swap_cores(send)).reshape(devices, part, width)

    counts = by_device(
        *call(
            lambda *r: count_kernel(*r, list_len=list_len),
            (place, slots),
            1,
            ((half, width), (half, width)),
            ((2 * half, width),),
            8_000_000,
        )
    )
    start_fields, *early = tell(
        jnp.concatenate([spread(share(atom_value)), spread(share(target_value))], axis=1),
        (place_first, place, own, share(atom_value), share(observed), templates, slots, coeffs,
         offsets, duals, weights, counts),
    )
    (place_first, place, own, mine, fixed, templates, slots, coeffs, offsets, duals,
     weights, counts) = early
    moved, e_target, keep, send = call(
        lambda *r: sweep_kernel(*r, list_len=list_len, beside=part),
        (place, place_first, start_fields, slots, coeffs, offsets, duals, templates, weights),
        2,
        (rule, (1, TEMPL), (half, width), (half, width)),
        ((2 * half, width), window, window),
        15_000_000,
    )
    sums = collect(jnp.concatenate([by_device(keep, send), counts], axis=1), count)
    sums = sums.reshape(2, 2, part, width)
    counted = sums[:, 1].reshape(piece, width) + 1.0

    def refresh(sums, before):
        stepped = jnp.clip((sums + before) / counted, 0.0, 1.0)
        return jnp.where(fixed == 1, before, stepped)

    mine = refresh(sums[:, 0].reshape(piece, width), mine)
    values = tell(spread(mine))
    moved, duals, keep, send = call(
        lambda *r: sweep_kernel(*r, list_len=list_len, beside=0),
        (place, values, slots, coeffs, offsets, duals, templates, weights, moved),
        1,
        (rule, rule, (half, width), (half, width)),
        ((2 * half, width), window),
        15_000_000,
    )
    values = tell(spread(refresh(collect(by_device(keep, send), count), mine)))
    energies, dual_next, consensus = call(
        lambda *r: energy_kernel(*r, list_len=list_len),
        (place, own, values, slots, coeffs, offsets, duals, templates, e_target, moved),
        2,
        ((1, 2 * TEMPL), rule, (atom_blk, width)),
        (window,),
        10_000_000,
    )
    energies = deal(jnp.broadcast_to(energies[None], (devices, 1, 2 * TEMPL)))
    energies = jnp.sum(energies, axis=(0, 1))
    e_value, e_target = energies[:TEMPL], energies[TEMPL:]
    weight_next = weight * jnp.exp(-LEARN_RATE * (e_value - e_target) / (e_value + e_target + 1.0))
    return consensus, dual_next.reshape(dual_value.shape), weight_next


def solution(mesh):
    in_specs = (
        P("blk", None),
        P("blk", None),
        P("blk", None),
        P(),
        P(),
        P(None, "grp", "blk"),
        P(None, "grp", "blk"),
        P("grp", "blk"),
        P(None, "grp", "blk"),
        P("grp", "blk"),
        P(),
    )
    out_specs = (P("blk", None), P(None, "grp", "blk"), P())
    return jax.shard_map(local, mesh=mesh, in_specs=in_specs, out_specs=out_specs, check_vma=False)
```
